128 devices in a mesh: slab: 8 (over z_hi, x), tile: 16 (over z_lo, y, core).
Axes of the slice: x: 4, y: 4, z: 4 (z_hi: 2, z_lo: 2; z = z_hi * 2 + z_lo), core: 2. Of those that a mesh axis runs over, the one named last changes fastest.
Arguments:
- state: float32 [512, 256, 1024], P('slab', 'tile'), may hold values from -6 to 6
- coeff: float32 [512, 256, 1024], P('slab', 'tile'), may hold values from 0.04 to 0.16
- target: float32 [512, 256, 1024], P('slab', 'tile'), may hold values from -6 to 6
- control: float32 [8, 256, 1024], P('slab', 'tile'), may hold values from -6 to 6
- multiplier: float32 [8, 256, 1024], P('slab', 'tile'), may hold values from -6 to 6
Outputs:
- final_state: float32 [512, 256, 1024], P('slab', 'tile')
- adjoint_start: float32 [512, 256, 1024], P('slab', 'tile')
- new_control: float32 [8, 256, 1024], P('slab', 'tile')
- new_multiplier: float32 [8, 256, 1024], P('slab', 'tile')
The draws below stay inside these ranges and needn't reach their ends.
All inputs are finite; a program needn't handle non-finite values.
Results may differ from the reference program's by a relative error of at most 0.00002.
Values sent between devices are 32-bit elements; how exact they have to be, the bound alone decides.
A program may use at most 128 MiB of HBM per device.

```python
import jax
import jax.numpy as jnp

CZ = 64
NY = 1024
NZ = 512
NX = 256
N_SLAB = 8


def levels(own_key, dims, cuts, least, high):
    level = 1.0
    for dim, parts in cuts:
        steps = jax.random.uniform(jax.random.fold_in(jax.random.fold_in(own_key, 6), dim), (parts,), jnp.float32, least / len(cuts), high / len(cuts))
        level = level * jnp.repeat(jnp.exp(steps), dims[dim] // parts).reshape((-1,) + (1,) * (len(dims) - 1 - dim))
    return level


def centred(key, shape, spread, most, pieces=(), dtype=jnp.bfloat16):
    gain = levels(key, shape, pieces, -0.22, 0.18) if pieces else 1.0
    values = jax.random.normal(key, shape, jnp.float32) * spread * gain
    return jnp.minimum(jnp.maximum(values, -most), most).astype(dtype)


def setup_inputs(seed: int = 0) -> dict:
    splits = jax.random.split(jax.random.key(seed), 6)
    state = centred(splits[0], (NZ, NX, NY), 1.0, 6.0, ((0, 8), (1, 16)), jnp.float32)
    coeff = jnp.clip(0.04 + 0.12 * jax.random.uniform(splits[1], (NZ, NX, NY), jnp.float32) ** levels(splits[1], (NZ, NX, NY), ((0, 8), (1, 16)), -0.2, 0.2), 0.04, 0.16)
    target = centred(splits[2], (NZ, NX, NY), 1.0, 6.0, ((0, 8), (1, 16)), jnp.float32)
    control = centred(splits[3], (N_SLAB, NX, NY), 1.0, 6.0, ((0, 8), (1, 16)), jnp.float32)
    multiplier = centred(splits[4], (N_SLAB, NX, NY), 1.0, 6.0, ((0, 8), (1, 16)), jnp.float32)
    return dict(state=state, coeff=coeff, target=target, control=control, multiplier=multiplier)


rho_step = 0.5
tau_step = 0.5


def ghost_lap(field, below_plane, above_plane):
    blocks = field.reshape(N_SLAB, CZ, NX, NY)
    upper = jnp.concatenate([blocks[:, 1:], above_plane[:, None]], axis=1).reshape(NZ, NX, NY)
    lower = jnp.concatenate([below_plane[:, None], blocks[:, :-1]], axis=1).reshape(NZ, NX, NY)
    padded = jnp.pad(field, ((0, 0), (1, 1), (1, 1)))
    beside = padded[:, 2:, 1:-1] + padded[:, :-2, 1:-1] + padded[:, 1:-1, 2:] + padded[:, 1:-1, :-2]
    return upper + lower + beside - 6.0 * field


def reference(state, coeff, target, control, multiplier):
    below_plane = jnp.roll(control, 1, axis=0)
    zero_plane = jnp.zeros_like(control)
    middle = state + coeff * ghost_lap(state, below_plane, control)
    final_state = middle + coeff * ghost_lap(middle, below_plane, control)
    adj_two = final_state - target
    adj_one = adj_two + ghost_lap(coeff * adj_two, zero_plane, zero_plane)
    adjoint_start = adj_one + ghost_lap(coeff * adj_one, zero_plane, zero_plane)
    fin_blocks = final_state.reshape(N_SLAB, CZ, NX, NY)
    flux = (coeff * (adj_one + adj_two)).reshape(N_SLAB, CZ, NX, NY)
    upper_trace = fin_blocks[:, -1]
    lower_trace = jnp.roll(fin_blocks[:, 0], -1, axis=0)
    grad = flux[:, -1] + jnp.roll(flux[:, 0], -1, axis=0)
    new_multiplier = multiplier + rho_step * (upper_trace - lower_trace)
    new_control = (control - tau_step * (grad + new_multiplier)) / (1.0 + tau_step)
    return final_state, adjoint_start, new_control, new_multiplier
```

```python
import functools

import jax
import jax.numpy as jnp
from jax import lax
from jax.experimental import pallas as pl
from jax.experimental.pallas import tpu as pltpu
from jax.sharding import PartitionSpec as P

rho_step = 0.5
tau_step = 0.5
LANES = 128
SUB = 8
CHUNK = 8
MESH = pl.DeviceIdType.MESH


def kernel(cz, nx, ny, n_slab, n_tile, unroll,
           state, coeff, target, control, multiplier,
           final, adj, new_control, new_multiplier,
           sp, mp, cf, tg, above, mult, below, flux, low_trace, low_flux,
           send, recv,
           sem_state, sem_coeff, sem_target, sem_small, sem_send, sem_recv, sem_slab_send, sem_slab_recv):
    yt_n = ny // LANES
    xt_n = nx // SUB
    pitch = nx + SUB
    plane = yt_n * pitch
    chunks = cz // CHUNK
    rows_n = sp.shape[0] * plane
    s2 = sp.reshape(rows_n, LANES)
    m2 = mp.reshape(rows_n, LANES)

    slab = lax.axis_index("slab")
    tile = lax.axis_index("tile")
    has = (tile > 0, tile < n_tile - 1)
    side_dev = ((slab, jnp.maximum(tile - 1, 0)), (slab, jnp.minimum(tile + 1, n_tile - 1)))
    up = (lax.rem(slab + 1, n_slab), tile)
    down = (lax.rem(slab + n_slab - 1, n_slab), tile)

    barrier = pltpu.get_barrier_semaphore()
    for side in range(2):
        @pl.when(has[side])
        def _():
            pl.semaphore_signal(barrier, inc=1, device_id=side_dev[side], device_id_type=MESH)
    pl.semaphore_signal(barrier, inc=1, device_id=up, device_id_type=MESH)
    pl.semaphore_signal(barrier, inc=1, device_id=down, device_id_type=MESH)

    def state_copy(k, yt):
        return pltpu.make_async_copy(
            state.at[pl.ds(k * CHUNK, CHUNK), :, pl.ds(yt * LANES, LANES)],
            sp.at[pl.ds(k * CHUNK + 1, CHUNK), yt, pl.ds(SUB, nx), :],
            sem_state.at[k, yt])

    def coeff_copy(k):
        return pltpu.make_async_copy(
            coeff.at[pl.ds(k * CHUNK, CHUNK)], cf.at[pl.ds(k * CHUNK, CHUNK)], sem_coeff.at[k])

    def target_copy(k):
        return pltpu.make_async_copy(
            target.at[pl.ds(k * CHUNK, CHUNK)], tg.at[pl.ds(k * CHUNK, CHUNK)], sem_target.at[k])

    above_copy = pltpu.make_async_copy(control, above, sem_small.at[0])
    mult_copy = pltpu.make_async_copy(multiplier, mult, sem_small.at[1])

    @pl.loop(0, chunks)
    def _(k):
        for yt in range(yt_n):
            state_copy(k, yt).start()
    above_copy.start()

    @pl.loop(0, chunks)
    def _(k):
        coeff_copy(k).start()

    @pl.loop(0, chunks)
    def _(k):
        target_copy(k).start()
    mult_copy.start()

    for side in range(2):
        @pl.when(jnp.logical_not(has[side]))
        def _():
            zeros = jnp.zeros((yt_n, LANES), jnp.float32)

            @pl.loop(1, cz + 1)
            def _(z):
                for field in (s2, m2):
                    field[pl.ds(z * plane + (SUB - 1 if side == 0 else SUB + nx), yt_n, stride=pitch), :] = zeros

    pl.semaphore_wait(barrier, 2 + has[0].astype(jnp.int32) + has[1].astype(jnp.int32))

    def slab_copy(i, src, dst, dev):
        return pltpu.make_async_remote_copy(
            src_ref=src, dst_ref=dst, send_sem=sem_slab_send.at[i], recv_sem=sem_slab_recv.at[i],
            device_id=dev, device_id_type=MESH)

    below_copy = slab_copy(0, control, below, up)
    trace_copy = slab_copy(1, final.at[pl.ds(0, 1)], low_trace, down)
    flux_copy = slab_copy(2, flux, low_flux, down)
    below_copy.start()

    def edge_copy(stage, side, k):
        return pltpu.make_async_remote_copy(
            src_ref=send.at[stage, side, pl.ds(k * CHUNK, CHUNK)],
            dst_ref=recv.at[stage, 1 - side, pl.ds(k * CHUNK, CHUNK)],
            send_sem=sem_send.at[stage, side, k], recv_sem=sem_recv.at[stage, 1 - side, k],
            device_id=side_dev[side], device_id_type=MESH)

    def send_edges(field, stage, k):
        @pl.loop(0, CHUNK)
        def _(i):
            z = k * CHUNK + i
            base = (z + 1) * plane
            send[stage, 0, z] = field[pl.ds(base + SUB, yt_n, stride=pitch), :]
            send[stage, 1, z] = field[pl.ds(base + SUB + nx - 1, yt_n, stride=pitch), :]
        for side in range(2):
            @pl.when(has[side])
            def _():
                edge_copy(stage, side, k).start()

    def take_halo(field, stage, k):
        for side in range(2):
            @pl.when(has[side])
            def _():
                edge_copy(stage, 1 - side, k).wait_recv()

                @pl.loop(0, CHUNK)
                def _(i):
                    z = k * CHUNK + i
                    base = (z + 1) * plane
                    row = SUB - 1 if side == 0 else SUB + nx
                    field[pl.ds(base + row, yt_n, stride=pitch), :] = recv[stage, side, z]

    lane = lax.broadcasted_iota(jnp.int32, (SUB, LANES), 1)
    first = lane == 0
    last = lane == LANES - 1
    zero = jnp.zeros((SUB, LANES), jnp.float32)

    def sweep(field, z, xt):
        base = (z + 1) * plane + SUB + xt * SUB
        mid = [field[pl.ds(base + yt * pitch, SUB), :] for yt in range(yt_n)]
        right = [pltpu.roll(v, 1, 1) for v in mid]
        left = [pltpu.roll(v, LANES - 1, 1) for v in mid]
        laps = []
        for yt in range(yt_n):
            at = base + yt * pitch
            y_minus = jnp.where(first, right[yt - 1] if yt else zero, right[yt])
            y_plus = jnp.where(last, left[yt + 1] if yt + 1 < yt_n else zero, left[yt])
            z_sum = field[pl.ds(at + plane, SUB), :] + field[pl.ds(at - plane, SUB), :]
            x_sum = field[pl.ds(at + 1, SUB), :] + field[pl.ds(at - 1, SUB), :]
            laps.append((z_sum + x_sum) + (y_minus + y_plus) - 6.0 * mid[yt])
        return mid, laps

    def planes(body):
        def run(k):
            @pl.loop(0, CHUNK, unroll=unroll)
            def _(i):
                body(k * CHUNK + i)
        return run

    def put(field, z, xt, yt, value):
        field[pl.ds((z + 1) * plane + SUB + xt * SUB + yt * pitch, SUB), :] = value

    def at(xt, yt):
        return pl.ds(xt * SUB, SUB), pl.ds(yt * LANES, LANES)

    @pl.loop(0, chunks)
    def _(k):
        for yt in range(yt_n):
            state_copy(k, yt).wait()
        send_edges(s2, 0, k)

    above_copy.wait()
    below_copy.wait_recv()
    for xt in range(xt_n):
        for yt in range(yt_n):
            lo = below[(0,) + at(xt, yt)]
            hi = above[(0,) + at(xt, yt)]
            for field in (s2, m2):
                put(field, -1, xt, yt, lo)
                put(field, cz, xt, yt, hi)

    @planes
    def middle(z):
        for xt in range(xt_n):
            mid, laps = sweep(s2, z, xt)
            for yt in range(yt_n):
                put(m2, z, xt, yt, mid[yt] + cf[(z,) + at(xt, yt)] * laps[yt])

    @pl.loop(0, chunks)
    def _(k):
        coeff_copy(k).wait()
        take_halo(s2, 0, k)
        middle(k)
        send_edges(m2, 1, k)

    for xt in range(xt_n):
        for yt in range(yt_n):
            put(s2, -1, xt, yt, zero)
            put(s2, cz, xt, yt, zero)

    @planes
    def finish(z):
        for xt in range(xt_n):
            mid, laps = sweep(m2, z, xt)
            for yt in range(yt_n):
                here = (z,) + at(xt, yt)
                c = cf[here]
                f = mid[yt] + c * laps[yt]
                final[here] = f
                two = f - tg[here]
                tg[here] = two
                put(s2, z, xt, yt, c * two)

    @pl.loop(0, chunks)
    def _(k):
        target_copy(k).wait()
        take_halo(m2, 1, k)
        finish(k)
        send_edges(s2, 2, k)

        @pl.when(k == 0)
        def _():
            trace_copy.start()

    for xt in range(xt_n):
        for yt in range(yt_n):
            put(m2, -1, xt, yt, zero)
            put(m2, cz, xt, yt, zero)

    mult_copy.wait()
    flux[0] = tg[0]
    new_control[0] = tg[cz - 1]

    @planes
    def back_one(z):
        for xt in range(xt_n):
            mid, laps = sweep(s2, z, xt)
            for yt in range(yt_n):
                here = (z,) + at(xt, yt)
                one = tg[here] + laps[yt]
                tg[here] = one
                put(m2, z, xt, yt, cf[here] * one)

    @pl.loop(0, chunks)
    def _(k):
        take_halo(s2, 2, k)
        back_one(k)
        send_edges(m2, 3, k)

        @pl.when(k == 0)
        def _():
            flux[0] = cf[0] * (tg[0] + flux[0])
            flux_copy.start()

    @planes
    def back_two(z):
        for xt in range(xt_n):
            mid, laps = sweep(m2, z, xt)
            for yt in range(yt_n):
                here = (z,) + at(xt, yt)
                adj[here] = tg[here] + laps[yt]

    @pl.loop(0, chunks)
    def _(k):
        take_halo(m2, 3, k)
        back_two(k)

    trace_copy.wait_recv()
    flux_copy.wait_recv()
    nm = mult[0] + rho_step * (final[cz - 1] - low_trace[0])
    new_multiplier[0] = nm
    grad = cf[cz - 1] * (tg[cz - 1] + new_control[0]) + low_flux[0]
    new_control[0] = (above[0] - tau_step * (grad + nm)) / (1.0 + tau_step)

    below_copy.wait_send()
    trace_copy.wait_send()
    flux_copy.wait_send()
    for side in range(2):
        @pl.when(has[side])
        def _():
            for stage in range(4):
                @pl.loop(0, chunks)
                def _(k):
                    edge_copy(stage, side, k).wait_send()


def iterate(n_slab, n_tile, state, coeff, target, control, multiplier, interpret=False, unroll=1):
    cz, nx, ny = state.shape
    yt_n = ny // LANES
    chunks = cz // CHUNK
    f32 = jnp.float32
    full = jax.ShapeDtypeStruct((cz, nx, ny), f32)
    face = jax.ShapeDtypeStruct((1, nx, ny), f32)
    padded = pltpu.VMEM((cz + 3, yt_n, nx + SUB, LANES), f32)
    natural = pltpu.VMEM((cz, nx, ny), f32)
    sheet = pltpu.VMEM((1, nx, ny), f32)
    edges = pltpu.VMEM((4, 2, cz, yt_n, LANES), f32)
    dma = pltpu.SemaphoreType.DMA
    return pl.pallas_call(
        functools.partial(kernel, cz, nx, ny, n_slab, n_tile, unroll),
        out_shape=(full, full, face, face),
        in_specs=[pl.BlockSpec(memory_space=pl.ANY)] * 5,
        out_specs=[pl.BlockSpec(memory_space=pltpu.VMEM)] * 4,
        scratch_shapes=[padded, padded, natural, natural] + [sheet] * 6 + [edges, edges]
        + [dma((chunks, yt_n)), dma((chunks,)), dma((chunks,)), dma((2,)),
           dma((4, 2, chunks)), dma((4, 2, chunks)), dma((3,)), dma((3,))],
        compiler_params=pltpu.CompilerParams(
            collective_id=0, has_side_effects=True, vmem_limit_bytes=56 * 2**20),
        interpret=interpret,
    )(state, coeff, target, control, multiplier)


def solution(mesh):
    spec = P("slab", "tile", None)
    run = functools.partial(iterate, mesh.shape["slab"], mesh.shape["tile"])
    return jax.shard_map(run, mesh=mesh, in_specs=(spec,) * 5, out_specs=(spec,) * 4, check_vma=False)
```

```python
import functools

import jax
import jax.numpy as jnp
from jax import lax
from jax.experimental import pallas as pl
from jax.experimental.pallas import tpu as pltpu
from jax.sharding import PartitionSpec as P

rho_step = 0.5
tau_step = 0.5
LANES = 128
SUB = 8
CHUNK = 16
UNROLL = 4
PARTS = 4
MESH = pl.DeviceIdType.MESH


def kernel(cz, nx, ny, n_slab, n_tile,
           state, coeff, target, control, multiplier,
           final, adj, new_control, new_multiplier,
           sp, mp, cf, tg, above, mult, below, flux, top_two, low_trace, low_flux,
           send, recv,
           sem_state, sem_coeff, sem_target, sem_small, sem_send, sem_recv, sem_slab_send, sem_slab_recv):
    yt_n = ny // LANES
    xt_n = nx // SUB
    pitch = nx + SUB
    plane = yt_n * pitch
    chunks = cz // CHUNK
    rows_n = sp.shape[0] * plane
    s2 = sp.reshape(rows_n, LANES)
    m2 = mp.reshape(rows_n, LANES)

    slab = lax.axis_index("slab")
    tile = lax.axis_index("tile")
    has = (tile > 0, tile < n_tile - 1)
    side_dev = ((slab, jnp.maximum(tile - 1, 0)), (slab, jnp.minimum(tile + 1, n_tile - 1)))
    up = (lax.rem(slab + 1, n_slab), tile)
    down = (lax.rem(slab + n_slab - 1, n_slab), tile)

    barrier = pltpu.get_barrier_semaphore()
    for side in range(2):
        @pl.when(has[side])
        def _():
            pl.semaphore_signal(barrier, inc=1, device_id=side_dev[side], device_id_type=MESH)
    pl.semaphore_signal(barrier, inc=1, device_id=up, device_id_type=MESH)
    pl.semaphore_signal(barrier, inc=1, device_id=down, device_id_type=MESH)

    def state_copy(k, yt):
        return pltpu.make_async_copy(
            state.at[pl.ds(k * CHUNK, CHUNK), :, pl.ds(yt * LANES, LANES)],
            sp.at[pl.ds(k * CHUNK + 1, CHUNK), yt, pl.ds(SUB, nx), :],
            sem_state.at[k, yt])

    def coeff_copy(k):
        return pltpu.make_async_copy(
            coeff.at[pl.ds(k * CHUNK, CHUNK)], cf.at[pl.ds(k * CHUNK, CHUNK)], sem_coeff.at[k])

    def target_copy(k):
        return pltpu.make_async_copy(
            target.at[pl.ds(k * CHUNK, CHUNK)], tg.at[pl.ds(k * CHUNK, CHUNK)], sem_target.at[k])

    above_copy = pltpu.make_async_copy(control, above, sem_small.at[0])
    mult_copy = pltpu.make_async_copy(multiplier, mult, sem_small.at[1])

    @pl.loop(0, chunks)
    def _(k):
        for yt in range(yt_n):
            state_copy(k, yt).start()
    above_copy.start()

    @pl.loop(0, chunks)
    def _(k):
        coeff_copy(k).start()

    @pl.loop(0, chunks)
    def _(k):
        target_copy(k).start()
    mult_copy.start()

    for side in range(2):
        @pl.when(jnp.logical_not(has[side]))
        def _():
            @pl.loop(0, cz)
            def _(z):
                for stage in range(4):
                    recv[stage, side, z] = jnp.zeros((yt_n, LANES), jnp.float32)

    pl.semaphore_wait(barrier, 2 + has[0].astype(jnp.int32) + has[1].astype(jnp.int32))

    def slab_copy(i, src, dst, dev):
        return pltpu.make_async_remote_copy(
            src_ref=src, dst_ref=dst, send_sem=sem_slab_send.at[i], recv_sem=sem_slab_recv.at[i],
            device_id=dev, device_id_type=MESH)

    below_copy = slab_copy(0, control, below, up)
    trace_copy = slab_copy(1, final.at[pl.ds(0, 1)], low_trace, down)
    flux_copy = slab_copy(2, flux, low_flux, down)
    below_copy.start()

    def edge_copy(stage, side, k):
        return pltpu.make_async_remote_copy(
            src_ref=send.at[stage, side, pl.ds(k * CHUNK, CHUNK)],
            dst_ref=recv.at[stage, 1 - side, pl.ds(k * CHUNK, CHUNK)],
            send_sem=sem_send.at[stage, side, k], recv_sem=sem_recv.at[stage, 1 - side, k],
            device_id=side_dev[side], device_id_type=MESH)

    def pack_edges(field, stage, z):
        base = (z + 1) * plane
        send[stage, 0, z] = field[pl.ds(base + SUB, yt_n, stride=pitch), :]
        send[stage, 1, z] = field[pl.ds(base + SUB + nx - 1, yt_n, stride=pitch), :]

    def send_edges(stage, k):
        for side in range(2):
            @pl.when(has[side])
            def _():
                edge_copy(stage, side, k).start()

    def wait_halo(stage, k):
        for side in range(2):
            @pl.when(has[side])
            def _():
                edge_copy(stage, 1 - side, k).wait_recv()

    def place_halo(field, stage, z):
        base = (z + 1) * plane
        field[pl.ds(base + SUB - 1, yt_n, stride=pitch), :] = recv[stage, 0, z]
        field[pl.ds(base + SUB + nx, yt_n, stride=pitch), :] = recv[stage, 1, z]

    lane = lax.broadcasted_iota(jnp.int32, (SUB, LANES), 1)
    first = lane == 0
    last = lane == LANES - 1
    zero = jnp.zeros((SUB, LANES), jnp.float32)

    def y_sums(field, z, xt):
        base = (z + 1) * plane + SUB + xt * SUB
        mid = [field[pl.ds(base + yt * pitch, SUB), :] for yt in range(yt_n)]
        right = [pltpu.roll(v, 1, 1) for v in mid]
        left = [pltpu.roll(v, LANES - 1, 1) for v in mid]
        return [jnp.where(first, right[yt - 1] if yt else zero, right[yt])
                + jnp.where(last, left[yt + 1] if yt + 1 < yt_n else zero, left[yt]) for yt in range(yt_n)]

    def center_and_lap(field, z, xt, yt, y_sum):
        at = (z + 1) * plane + SUB + xt * SUB + yt * pitch
        mid = field[pl.ds(at, SUB), :]
        z_sum = field[pl.ds(at + plane, SUB), :] + field[pl.ds(at - plane, SUB), :]
        x_sum = field[pl.ds(at + 1, SUB), :] + field[pl.ds(at - 1, SUB), :]
        return mid, (z_sum + x_sum) + y_sum - 6.0 * mid

    def put(field, z, xt, yt, value):
        field[pl.ds((z + 1) * plane + SUB + xt * SUB + yt * pitch, SUB), :] = value

    def at(xt, yt):
        return pl.ds(xt * SUB, SUB), pl.ds(yt * LANES, LANES)

    def sweep(field, stage_in, emit, before, after, out=None, stage_out=None):
        def one_plane(z, sums):
            place_halo(field, stage_in, z)
            for xt in range(xt_n):
                ahead = y_sums(field, z, xt + 1) if xt + 1 < xt_n else y_sums(field, z + 1, 0)
                for yt in range(yt_n):
                    emit(z, xt, yt, *center_and_lap(field, z, xt, yt, sums[yt]))
                sums = ahead
            if out is not None:
                pack_edges(out, stage_out, z)
            return sums

        def one_chunk(k, sums):
            before(k)
            wait_halo(stage_in, k)
            sums = lax.fori_loop(0, CHUNK, lambda i, c: one_plane(k * CHUNK + i, c), sums, unroll=UNROLL)
            if out is not None:
                send_edges(stage_out, k)
            after(k)
            return sums

        lax.fori_loop(0, chunks, one_chunk, y_sums(field, 0, 0))

    def nothing(k):
        pass

    @pl.loop(0, chunks)
    def _(k):
        for yt in range(yt_n):
            state_copy(k, yt).wait()

        @pl.loop(0, CHUNK, unroll=4)
        def _(i):
            pack_edges(s2, 0, k * CHUNK + i)
        send_edges(0, k)

    above_copy.wait()
    below_copy.wait_recv()
    for xt in range(xt_n):
        for yt in range(yt_n):
            lo = below[(0,) + at(xt, yt)]
            hi = above[(0,) + at(xt, yt)]
            for field in (s2, m2):
                put(field, -1, xt, yt, lo)
                put(field, cz, xt, yt, hi)

    def middle(z, xt, yt, mid, lap):
        put(m2, z, xt, yt, mid + cf[(z,) + at(xt, yt)] * lap)

    sweep(s2, 0, middle, lambda k: coeff_copy(k).wait(), nothing, m2, 1)

    for xt in range(xt_n):
        for yt in range(yt_n):
            put(s2, -1, xt, yt, zero)
            put(s2, cz, xt, yt, zero)

    def finish(z, xt, yt, mid, lap):
        here = (z,) + at(xt, yt)
        c = cf[here]
        f = mid + c * lap
        final[here] = f
        two = f - tg[here]
        tg[here] = two
        put(s2, z, xt, yt, c * two)

    def send_trace(k):
        @pl.when(k == 0)
        def _():
            trace_copy.start()

    sweep(m2, 1, finish, lambda k: target_copy(k).wait(), send_trace, s2, 2)

    for xt in range(xt_n):
        for yt in range(yt_n):
            put(m2, -1, xt, yt, zero)
            put(m2, cz, xt, yt, zero)

    flux[0] = tg[0]
    top_two[0] = tg[cz - 1]

    def back_one(z, xt, yt, mid, lap):
        here = (z,) + at(xt, yt)
        one = tg[here] + lap
        tg[here] = one
        put(m2, z, xt, yt, cf[here] * one)

    def send_flux(k):
        @pl.when(k == 0)
        def _():
            flux[0] = cf[0] * (tg[0] + flux[0])
            flux_copy.start()

    sweep(s2, 2, back_one, nothing, send_flux, m2, 3)

    def back_two(z, xt, yt, mid, lap):
        here = (z,) + at(xt, yt)
        adj[here] = tg[here] + lap

    sweep(m2, 3, back_two, nothing, nothing)

    mult_copy.wait()
    trace_copy.wait_recv()
    flux_copy.wait_recv()
    nm = mult[0] + rho_step * (final[cz - 1] - low_trace[0])
    new_multiplier[0] = nm
    grad = cf[cz - 1] * (tg[cz - 1] + top_two[0]) + low_flux[0]
    new_control[0] = (above[0] - tau_step * (grad + nm)) / (1.0 + tau_step)

    below_copy.wait_send()
    trace_copy.wait_send()
    flux_copy.wait_send()
    for side in range(2):
        @pl.when(has[side])
        def _():
            for stage in range(4):
                @pl.loop(0, chunks)
                def _(k):
                    edge_copy(stage, side, k).wait_send()


def write_out(parts, *refs):
    sem = refs[-1]
    n = (len(refs) - 1) // 2
    copies = []
    for i in range(n):
        planes = refs[i].shape[0]
        step = max(planes // parts, 1)
        for j in range(planes // step):
            span = pl.ds(j * step, step)
            copies.append(pltpu.make_async_copy(refs[i].at[span], refs[n + i].at[span], sem.at[i, j]))
    for copy in copies:
        copy.start()
    for copy in copies:
        copy.wait()


def iterate(n_slab, n_tile, state, coeff, target, control, multiplier):
    cz, nx, ny = state.shape
    yt_n = ny // LANES
    chunks = cz // CHUNK
    f32 = jnp.float32
    padded = pltpu.VMEM((cz + 3, yt_n, nx + SUB, LANES), f32)
    natural = pltpu.VMEM((cz, nx, ny), f32)
    sheet = pltpu.VMEM((1, nx, ny), f32)
    edges = pltpu.VMEM((4, 2, cz, yt_n, LANES), f32)
    dma = pltpu.SemaphoreType.DMA
    arrays = [pltpu.with_memory_space_constraint(a, pltpu.HBM) for a in (state, coeff, target, control, multiplier)]
    results = pl.pallas_call(
        functools.partial(kernel, cz, nx, ny, n_slab, n_tile),
        out_shape=(natural, natural, sheet, sheet),
        in_specs=[pl.BlockSpec(memory_space=pltpu.HBM)] * 5,
        out_specs=[pl.BlockSpec(memory_space=pltpu.VMEM)] * 4,
        scratch_shapes=[padded, padded, natural, natural] + [sheet] * 7 + [edges, edges]
        + [dma((chunks, yt_n)), dma((chunks,)), dma((chunks,)), dma((2,)),
           dma((4, 2, chunks)), dma((4, 2, chunks)), dma((3,)), dma((3,))],
        compiler_params=pltpu.CompilerParams(
            collective_id=0, has_side_effects=True, vmem_limit_bytes=40 * 2**20),
    )(*arrays)
    full = jax.ShapeDtypeStruct((cz, nx, ny), f32)
    face = jax.ShapeDtypeStruct((1, nx, ny), f32)
    return pl.pallas_call(
        functools.partial(write_out, PARTS),
        out_shape=(full, full, face, face),
        in_specs=[pl.BlockSpec(memory_space=pltpu.VMEM)] * 4,
        out_specs=[pl.BlockSpec(memory_space=pl.ANY)] * 4,
        scratch_shapes=[dma((4, PARTS))],
        compiler_params=pltpu.CompilerParams(vmem_limit_bytes=16 * 2**20),
    )(*results)


def solution(mesh):
    spec = P("slab", "tile", None)
    run = functools.partial(iterate, mesh.shape["slab"], mesh.shape["tile"])
    return jax.shard_map(run, mesh=mesh, in_specs=(spec,) * 5, out_specs=(spec,) * 4, check_vma=False)
```

```python
import functools

import jax
import jax.numpy as jnp
from jax import lax
from jax.experimental import pallas as pl
from jax.experimental.pallas import tpu as pltpu
from jax.sharding import PartitionSpec as P

rho_step = 0.5
tau_step = 0.5
LANES = 128
SUB = 8
CHUNK = 16
GROUP = 4
BY_DOT = 2
PARTS = 4
MESH = pl.DeviceIdType.MESH


def kernel(cz, nx, ny, n_slab, n_tile,
           state, coeff, target, control, multiplier,
           final, adj, new_control, new_multiplier,
           sp, mp, cf, tg, above, mult, below, flux, top_two, low_trace, low_flux,
           send, recv, band, dots_a, dots_b,
           sem_state, sem_coeff, sem_target, sem_small, sem_send, sem_recv, sem_slab_send, sem_slab_recv):
    yt_n = ny // LANES
    xt_n = nx // SUB
    pitch = nx + SUB
    plane = yt_n * pitch
    chunks = cz // CHUNK
    rows_n = sp.shape[0] * plane
    s2 = sp.reshape(rows_n, LANES)
    m2 = mp.reshape(rows_n, LANES)

    slab = lax.axis_index("slab")
    tile = lax.axis_index("tile")
    has = (tile > 0, tile < n_tile - 1)
    side_dev = ((slab, jnp.maximum(tile - 1, 0)), (slab, jnp.minimum(tile + 1, n_tile - 1)))
    up = (lax.rem(slab + 1, n_slab), tile)
    down = (lax.rem(slab + n_slab - 1, n_slab), tile)

    barrier = pltpu.get_barrier_semaphore()
    for side in range(2):
        @pl.when(has[side])
        def _():
            pl.semaphore_signal(barrier, inc=1, device_id=side_dev[side], device_id_type=MESH)
    pl.semaphore_signal(barrier, inc=1, device_id=up, device_id_type=MESH)
    pl.semaphore_signal(barrier, inc=1, device_id=down, device_id_type=MESH)

    def state_copy(k, yt):
        return pltpu.make_async_copy(
            state.at[pl.ds(k * CHUNK, CHUNK), :, pl.ds(yt * LANES, LANES)],
            sp.at[pl.ds(k * CHUNK + 1, CHUNK), yt, pl.ds(SUB, nx), :],
            sem_state.at[k, yt])

    def coeff_copy(k):
        return pltpu.make_async_copy(
            coeff.at[pl.ds(k * CHUNK, CHUNK)], cf.at[pl.ds(k * CHUNK, CHUNK)], sem_coeff.at[k])

    def target_copy(k):
        return pltpu.make_async_copy(
            target.at[pl.ds(k * CHUNK, CHUNK)], tg.at[pl.ds(k * CHUNK, CHUNK)], sem_target.at[k])

    above_copy = pltpu.make_async_copy(control, above, sem_small.at[0])
    mult_copy = pltpu.make_async_copy(multiplier, mult, sem_small.at[1])

    @pl.loop(0, chunks)
    def _(k):
        for yt in range(yt_n):
            state_copy(k, yt).start()
    above_copy.start()

    @pl.loop(0, chunks)
    def _(k):
        coeff_copy(k).start()

    @pl.loop(0, chunks)
    def _(k):
        target_copy(k).start()
    mult_copy.start()

    for side in range(2):
        @pl.when(jnp.logical_not(has[side]))
        def _():
            @pl.loop(0, cz)
            def _(z):
                for stage in range(4):
                    recv[stage, side, z] = jnp.zeros((yt_n, LANES), jnp.float32)

    pl.semaphore_wait(barrier, 2 + has[0].astype(jnp.int32) + has[1].astype(jnp.int32))

    def slab_copy(i, src, dst, dev):
        return pltpu.make_async_remote_copy(
            src_ref=src, dst_ref=dst, send_sem=sem_slab_send.at[i], recv_sem=sem_slab_recv.at[i],
            device_id=dev, device_id_type=MESH)

    below_copy = slab_copy(0, control, below, up)
    trace_copy = slab_copy(1, final.at[pl.ds(0, 1)], low_trace, down)
    flux_copy = slab_copy(2, flux, low_flux, down)
    below_copy.start()

    def edge_copy(stage, side, k):
        return pltpu.make_async_remote_copy(
            src_ref=send.at[stage, side, pl.ds(k * CHUNK, CHUNK)],
            dst_ref=recv.at[stage, 1 - side, pl.ds(k * CHUNK, CHUNK)],
            send_sem=sem_send.at[stage, side, k], recv_sem=sem_recv.at[stage, 1 - side, k],
            device_id=side_dev[side], device_id_type=MESH)

    def pack_edges(field, stage, z):
        base = (z + 1) * plane
        send[stage, 0, z] = field[pl.ds(base + SUB, yt_n, stride=pitch), :]
        send[stage, 1, z] = field[pl.ds(base + SUB + nx - 1, yt_n, stride=pitch), :]

    def send_edges(stage, k):
        for side in range(2):
            @pl.when(has[side])
            def _():
                edge_copy(stage, side, k).start()

    def wait_halo(stage, k):
        for side in range(2):
            @pl.when(has[side])
            def _():
                edge_copy(stage, 1 - side, k).wait_recv()

    def place_halo(field, stage, z):
        base = (z + 1) * plane
        field[pl.ds(base + SUB - 1, yt_n, stride=pitch), :] = recv[stage, 0, z]
        field[pl.ds(base + SUB + nx, yt_n, stride=pitch), :] = recv[stage, 1, z]

    lane = lax.broadcasted_iota(jnp.int32, (SUB, LANES), 1)
    first = lane == 0
    last = lane == LANES - 1
    zero = jnp.zeros((SUB, LANES), jnp.float32)

    def y_sums(field, z, xt):
        base = (z + 1) * plane + SUB + xt * SUB
        mid = [field[pl.ds(base + yt * pitch, SUB), :] for yt in range(yt_n)]
        right = [pltpu.roll(v, 1, 1) for v in mid]
        left = [pltpu.roll(v, LANES - 1, 1) for v in mid]
        return [jnp.where(first, right[yt - 1] if yt else zero, right[yt])
                + jnp.where(last, left[yt + 1] if yt + 1 < yt_n else zero, left[yt]) for yt in range(yt_n)]

    row = lax.rem(lax.broadcasted_iota(jnp.int32, (2 * LANES, LANES), 0), LANES)
    col = lax.broadcasted_iota(jnp.int32, (2 * LANES, LANES), 1)
    swap = jnp.logical_or(jnp.logical_and(row == LANES - 1, col == 0), jnp.logical_and(row == 0, col == LANES - 1))
    band[:, pl.ds(0, LANES)] = jnp.where(jnp.abs(row - col) == 1, 1.0, 0.0).astype(jnp.bfloat16)
    band[:, pl.ds(LANES, LANES)] = jnp.where(swap, 1.0, 0.0).astype(jnp.bfloat16)
    lower_half = lane < LANES // 2

    def dot_sums(field, z, to):
        rows = []
        for p in range(BY_DOT):
            base = (z + p + 1) * plane + SUB
            for yt in range(yt_n):
                mid = field[pl.ds(base + yt * pitch, nx), :]
                high = mid.astype(jnp.bfloat16)
                low = (mid - high.astype(jnp.float32)).astype(jnp.bfloat16)
                rows.append(jnp.concatenate([high, low], axis=1))
        to[...] = jnp.dot(jnp.concatenate(rows, axis=0), band[...], preferred_element_type=jnp.float32)

    def put(field, z, xt, yt, value):
        field[pl.ds((z + 1) * plane + SUB + xt * SUB + yt * pitch, SUB), :] = value

    def at(xt, yt):
        return pl.ds(xt * SUB, SUB), pl.ds(yt * LANES, LANES)

    groups = cz // GROUP

    def sweep(field, stage_in, emit, before, after, out=None, stage_out=None):
        def one_group(g, have, make):
            z = g * GROUP
            for p in range(GROUP):
                place_halo(field, stage_in, z + p)
            dot_sums(field, lax.rem(g + 1, groups) * GROUP, make)
            for xt in range(xt_n):
                rolled = {p: y_sums(field, z + p, xt) for p in range(BY_DOT, GROUP)}

                def piece(p, yt, part):
                    return have[pl.ds((p * yt_n + yt) * nx + xt * SUB, SUB), pl.ds(part * LANES, LANES)]
                outer = {(p, yt): piece(p, yt, 1) for p in range(BY_DOT) for yt in range(yt_n)}
                for yt in range(yt_n):
                    at = (z + 1) * plane + SUB + xt * SUB + yt * pitch
                    mid = [field[pl.ds(at + (p - 1) * plane, SUB), :] for p in range(GROUP + 2)]
                    for p in range(GROUP):
                        x_sum = field[pl.ds(at + p * plane + 1, SUB), :] + field[pl.ds(at + p * plane - 1, SUB), :]
                        if p < BY_DOT:
                            y_sum = piece(p, yt, 0) + jnp.where(
                                lower_half, outer.get((p, yt - 1), zero), outer.get((p, yt + 1), zero))
                        else:
                            y_sum = rolled[p][yt]
                        lap = ((mid[p] + mid[p + 2]) + x_sum) + y_sum - 6.0 * mid[p + 1]
                        emit(z + p, xt, yt, mid[p + 1], lap)
            if out is not None:
                for p in range(GROUP):
                    pack_edges(out, stage_out, z + p)

        dot_sums(field, 0, dots_a)

        @pl.loop(0, chunks)
        def _(k):
            before(k)
            wait_halo(stage_in, k)

            @pl.loop(0, CHUNK // GROUP // 2)
            def _(i):
                g = k * (CHUNK // GROUP) + 2 * i
                one_group(g, dots_a, dots_b)
                one_group(g + 1, dots_b, dots_a)
            if out is not None:
                send_edges(stage_out, k)
            after(k)

    def nothing(k):
        pass

    @pl.loop(0, chunks)
    def _(k):
        for yt in range(yt_n):
            state_copy(k, yt).wait()

        @pl.loop(0, CHUNK, unroll=4)
        def _(i):
            pack_edges(s2, 0, k * CHUNK + i)
        send_edges(0, k)

    above_copy.wait()
    below_copy.wait_recv()
    for xt in range(xt_n):
        for yt in range(yt_n):
            lo = below[(0,) + at(xt, yt)]
            hi = above[(0,) + at(xt, yt)]
            for field in (s2, m2):
                put(field, -1, xt, yt, lo)
                put(field, cz, xt, yt, hi)

    def middle(z, xt, yt, mid, lap):
        put(m2, z, xt, yt, mid + cf[(z,) + at(xt, yt)] * lap)

    sweep(s2, 0, middle, lambda k: coeff_copy(k).wait(), nothing, m2, 1)

    for xt in range(xt_n):
        for yt in range(yt_n):
            put(s2, -1, xt, yt, zero)
            put(s2, cz, xt, yt, zero)

    def finish(z, xt, yt, mid, lap):
        here = (z,) + at(xt, yt)
        c = cf[here]
        f = mid + c * lap
        final[here] = f
        two = f - tg[here]
        tg[here] = two
        put(s2, z, xt, yt, c * two)

    def send_trace(k):
        @pl.when(k == 0)
        def _():
            trace_copy.start()

    sweep(m2, 1, finish, lambda k: target_copy(k).wait(), send_trace, s2, 2)

    for xt in range(xt_n):
        for yt in range(yt_n):
            put(m2, -1, xt, yt, zero)
            put(m2, cz, xt, yt, zero)

    flux[0] = tg[0]
    top_two[0] = tg[cz - 1]

    def back_one(z, xt, yt, mid, lap):
        here = (z,) + at(xt, yt)
        one = tg[here] + lap
        tg[here] = one
        put(m2, z, xt, yt, cf[here] * one)

    def send_flux(k):
        @pl.when(k == 0)
        def _():
            flux[0] = cf[0] * (tg[0] + flux[0])
            flux_copy.start()

    sweep(s2, 2, back_one, nothing, send_flux, m2, 3)

    def back_two(z, xt, yt, mid, lap):
        here = (z,) + at(xt, yt)
        adj[here] = tg[here] + lap

    sweep(m2, 3, back_two, nothing, nothing)

    mult_copy.wait()
    trace_copy.wait_recv()
    flux_copy.wait_recv()
    nm = mult[0] + rho_step * (final[cz - 1] - low_trace[0])
    new_multiplier[0] = nm
    grad = cf[cz - 1] * (tg[cz - 1] + top_two[0]) + low_flux[0]
    new_control[0] = (above[0] - tau_step * (grad + nm)) / (1.0 + tau_step)

    below_copy.wait_send()
    trace_copy.wait_send()
    flux_copy.wait_send()
    for side in range(2):
        @pl.when(has[side])
        def _():
            for stage in range(4):
                @pl.loop(0, chunks)
                def _(k):
                    edge_copy(stage, side, k).wait_send()


def write_out(parts, *refs):
    sem = refs[-1]
    n = (len(refs) - 1) // 2
    copies = []
    for i in range(n):
        planes = refs[i].shape[0]
        step = max(planes // parts, 1)
        for j in range(planes // step):
            span = pl.ds(j * step, step)
            copies.append(pltpu.make_async_copy(refs[i].at[span], refs[n + i].at[span], sem.at[i, j]))
    for copy in copies:
        copy.start()
    for copy in copies:
        copy.wait()


def iterate(n_slab, n_tile, state, coeff, target, control, multiplier):
    cz, nx, ny = state.shape
    yt_n = ny // LANES
    chunks = cz // CHUNK
    f32 = jnp.float32
    padded = pltpu.VMEM((cz + 3, yt_n, nx + SUB, LANES), f32)
    natural = pltpu.VMEM((cz, nx, ny), f32)
    sheet = pltpu.VMEM((1, nx, ny), f32)
    edges = pltpu.VMEM((4, 2, cz, yt_n, LANES), f32)
    dots = pltpu.VMEM((BY_DOT * yt_n * nx, 2 * LANES), f32)
    dma = pltpu.SemaphoreType.DMA
    arrays = [pltpu.with_memory_space_constraint(a, pltpu.HBM) for a in (state, coeff, target, control, multiplier)]
    results = pl.pallas_call(
        functools.partial(kernel, cz, nx, ny, n_slab, n_tile),
        out_shape=(natural, natural, sheet, sheet),
        in_specs=[pl.BlockSpec(memory_space=pltpu.HBM)] * 5,
        out_specs=[pl.BlockSpec(memory_space=pltpu.VMEM)] * 4,
        scratch_shapes=[padded, padded, natural, natural] + [sheet] * 7 + [edges, edges, pltpu.VMEM((2 * LANES, 2 * LANES), jnp.bfloat16), dots, dots]
        + [dma((chunks, yt_n)), dma((chunks,)), dma((chunks,)), dma((2,)),
           dma((4, 2, chunks)), dma((4, 2, chunks)), dma((3,)), dma((3,))],
        compiler_params=pltpu.CompilerParams(
            collective_id=0, has_side_effects=True, vmem_limit_bytes=40 * 2**20),
    )(*arrays)
    full = jax.ShapeDtypeStruct((cz, nx, ny), f32)
    face = jax.ShapeDtypeStruct((1, nx, ny), f32)
    return pl.pallas_call(
        functools.partial(write_out, PARTS),
        out_shape=(full, full, face, face),
        in_specs=[pl.BlockSpec(memory_space=pltpu.VMEM)] * 4,
        out_specs=[pl.BlockSpec(memory_space=pl.ANY)] * 4,
        scratch_shapes=[dma((4, PARTS))],
        compiler_params=pltpu.CompilerParams(vmem_limit_bytes=16 * 2**20),
    )(*results)


def solution(mesh):
    spec = P("slab", "tile", None)
    run = functools.partial(iterate, mesh.shape["slab"], mesh.shape["tile"])
    return jax.shard_map(run, mesh=mesh, in_specs=(spec,) * 5, out_specs=(spec,) * 4, check_vma=False)
```

```python
import functools

import jax
import jax.numpy as jnp
from jax import lax
from jax.experimental import pallas as pl
from jax.experimental.pallas import tpu as pltpu
from jax.sharding import PartitionSpec as P

rho_step = 0.5
tau_step = 0.5
LANES = 128
SUB = 8
CHUNK = 8
GROUP = 4
BY_DOT = 3
PARTS = 4
UNITS = 2
NY = 1024
NX_LOCAL = 16
MESH = pl.DeviceIdType.MESH


def kernel(cz, nx, ny, n_slab, n_tile, accumulators,
           state, coeff, target, control, multiplier,
           final, adj, new_control, new_multiplier,
           sp, mp, cf, tg, above, mult, below, flux, top_two, low_trace, low_flux,
           send, recv, band,
           sem_state, sem_coeff, sem_target, sem_small, sem_send, sem_recv, sem_slab_send, sem_slab_recv):
    yt_n = ny // LANES
    xt_n = nx // SUB
    pitch = nx + SUB
    plane = yt_n * pitch
    chunks = cz // CHUNK
    rows_n = sp.shape[0] * plane
    s2 = sp.reshape(rows_n, LANES)
    m2 = mp.reshape(rows_n, LANES)

    slab = lax.axis_index("slab")
    tile = lax.axis_index("tile")
    has = (tile > 0, tile < n_tile - 1)
    side_dev = ((slab, jnp.maximum(tile - 1, 0)), (slab, jnp.minimum(tile + 1, n_tile - 1)))
    up = (lax.rem(slab + 1, n_slab), tile)
    down = (lax.rem(slab + n_slab - 1, n_slab), tile)

    barrier = pltpu.get_barrier_semaphore()
    for side in range(2):
        @pl.when(has[side])
        def _():
            pl.semaphore_signal(barrier, inc=1, device_id=side_dev[side], device_id_type=MESH)
    pl.semaphore_signal(barrier, inc=1, device_id=up, device_id_type=MESH)
    pl.semaphore_signal(barrier, inc=1, device_id=down, device_id_type=MESH)

    def state_copy(k, yt):
        return pltpu.make_async_copy(
            state.at[pl.ds(k * CHUNK, CHUNK), :, pl.ds(yt * LANES, LANES)],
            sp.at[pl.ds(k * CHUNK + 1, CHUNK), yt, pl.ds(SUB, nx), :],
            sem_state.at[k, yt])

    def coeff_copy(k):
        return pltpu.make_async_copy(
            coeff.at[pl.ds(k * CHUNK, CHUNK)], cf.at[pl.ds(k * CHUNK, CHUNK)], sem_coeff.at[k])

    def target_copy(k):
        return pltpu.make_async_copy(
            target.at[pl.ds(k * CHUNK, CHUNK)], tg.at[pl.ds(k * CHUNK, CHUNK)], sem_target.at[k])

    above_copy = pltpu.make_async_copy(control, above, sem_small.at[0])
    mult_copy = pltpu.make_async_copy(multiplier, mult, sem_small.at[1])

    @pl.loop(0, chunks)
    def _(k):
        for yt in range(yt_n):
            state_copy(k, yt).start()
    above_copy.start()

    @pl.loop(0, chunks)
    def _(k):
        coeff_copy(k).start()

    @pl.loop(0, chunks)
    def _(k):
        target_copy(k).start()
    mult_copy.start()

    for side in range(2):
        @pl.when(jnp.logical_not(has[side]))
        def _():
            @pl.loop(0, cz)
            def _(z):
                for stage in range(4):
                    recv[stage, side, z] = jnp.zeros((yt_n, LANES), jnp.float32)

    pl.semaphore_wait(barrier, 2 + has[0].astype(jnp.int32) + has[1].astype(jnp.int32))

    def slab_copy(i, src, dst, dev):
        return pltpu.make_async_remote_copy(
            src_ref=src, dst_ref=dst, send_sem=sem_slab_send.at[i], recv_sem=sem_slab_recv.at[i],
            device_id=dev, device_id_type=MESH)

    below_copy = slab_copy(0, control, below, up)
    trace_copy = slab_copy(1, final.at[pl.ds(0, 1)], low_trace, down)
    flux_copy = slab_copy(2, flux, low_flux, down)
    below_copy.start()

    def edge_copy(stage, side, k):
        return pltpu.make_async_remote_copy(
            src_ref=send.at[stage, side, pl.ds(k * CHUNK, CHUNK)],
            dst_ref=recv.at[stage, 1 - side, pl.ds(k * CHUNK, CHUNK)],
            send_sem=sem_send.at[stage, side, k], recv_sem=sem_recv.at[stage, 1 - side, k],
            device_id=side_dev[side], device_id_type=MESH)

    def pack_edges(field, stage, z):
        base = (z + 1) * plane
        send[stage, 0, z] = field[pl.ds(base + SUB, yt_n, stride=pitch), :]
        send[stage, 1, z] = field[pl.ds(base + SUB + nx - 1, yt_n, stride=pitch), :]

    def send_edges(stage, k):
        for side in range(2):
            @pl.when(has[side])
            def _():
                edge_copy(stage, side, k).start()

    def wait_halo(stage, k):
        for side in range(2):
            @pl.when(has[side])
            def _():
                edge_copy(stage, 1 - side, k).wait_recv()

    def place_halo(field, stage, z):
        base = (z + 1) * plane
        field[pl.ds(base + SUB - 1, yt_n, stride=pitch), :] = recv[stage, 0, z]
        field[pl.ds(base + SUB + nx, yt_n, stride=pitch), :] = recv[stage, 1, z]

    lane = lax.broadcasted_iota(jnp.int32, (SUB, LANES), 1)
    first = lane == 0
    last = lane == LANES - 1
    zero = jnp.zeros((SUB, LANES), jnp.float32)

    def y_sums(field, z, xt):
        base = (z + 1) * plane + SUB + xt * SUB
        mid = [field[pl.ds(base + yt * pitch, SUB), :] for yt in range(yt_n)]
        right = [pltpu.roll(v, 1, 1) for v in mid]
        left = [pltpu.roll(v, LANES - 1, 1) for v in mid]
        return [jnp.where(first, right[yt - 1] if yt else zero, right[yt])
                + jnp.where(last, left[yt + 1] if yt + 1 < yt_n else zero, left[yt]) for yt in range(yt_n)]

    row = lax.rem(lax.broadcasted_iota(jnp.int32, (2 * LANES, LANES), 0), LANES)
    col = lax.broadcasted_iota(jnp.int32, (2 * LANES, LANES), 1)
    swap = jnp.logical_or(jnp.logical_and(row == LANES - 1, col == 0), jnp.logical_and(row == 0, col == LANES - 1))
    band[:, pl.ds(0, LANES)] = jnp.where(jnp.abs(row - col) == 1, 1.0, 0.0).astype(jnp.bfloat16)
    band[:, pl.ds(LANES, LANES)] = jnp.where(swap, 1.0, 0.0).astype(jnp.bfloat16)
    lower_half = lax.broadcasted_iota(jnp.int32, (nx, LANES), 1) < LANES // 2
    no_piece = jnp.zeros((nx, LANES), jnp.float32)

    def start_dots(field, z, accs, load=False):
        for p in range(BY_DOT):
            base = (z + p + 1) * plane + SUB
            for yt in range(yt_n):
                mid = field[pl.ds(base + yt * pitch, nx), :]
                high = mid.astype(jnp.bfloat16)
                low = (mid - high.astype(jnp.float32)).astype(jnp.bfloat16)
                pltpu.matmul_acc_lhs(accs[p * yt_n + yt], jnp.concatenate([high, low], axis=1),
                                     load_staged_rhs=0 if load and p * yt_n + yt < UNITS else None)

    def take_dots(accs, p):
        both = [pltpu.matmul_pop(accs[p * yt_n + yt]) for yt in range(yt_n)]
        sums = []
        for yt in range(yt_n):
            lower = both[yt - 1][:, LANES:] if yt else no_piece
            upper = both[yt + 1][:, LANES:] if yt + 1 < yt_n else no_piece
            sums.append(both[yt][:, :LANES] + jnp.where(lower_half, lower, upper))
        return [[v[xt * SUB:(xt + 1) * SUB] for v in sums] for xt in range(xt_n)]

    def put(field, z, xt, yt, value):
        field[pl.ds((z + 1) * plane + SUB + xt * SUB + yt * pitch, SUB), :] = value

    def at(xt, yt):
        return pl.ds(xt * SUB, SUB), pl.ds(yt * LANES, LANES)

    groups = cz // GROUP

    def sweep(field, stage_in, emit, before, after, out=None, stage_out=None):
        def one_group(g, have, make):
            z = g * GROUP
            for p in range(GROUP):
                place_halo(field, stage_in, z + p)
            start_dots(field, lax.rem(g + 1, groups) * GROUP, make)
            for p in range(GROUP):
                if p < BY_DOT:
                    sums = take_dots(have, p)
                else:
                    sums = [y_sums(field, z + p, xt) for xt in range(xt_n)]
                for yt in range(yt_n):
                    for xt in range(xt_n):
                        at = (z + p + 1) * plane + SUB + xt * SUB + yt * pitch
                        mid = field[pl.ds(at, SUB), :]
                        x_sum = field[pl.ds(at + 1, SUB), :] + field[pl.ds(at - 1, SUB), :]
                        z_sum = field[pl.ds(at + plane, SUB), :] + field[pl.ds(at - plane, SUB), :]
                        emit(z + p, xt, yt, mid, (z_sum + x_sum) + sums[xt][yt] - 6.0 * mid)
            if out is not None:
                for p in range(GROUP):
                    pack_edges(out, stage_out, z + p)

        def with_accumulators(*accs):
            first, second = accs[:BY_DOT * yt_n], accs[BY_DOT * yt_n:]
            for unit in range(UNITS):
                pltpu.matmul_push_rhs(band[...], 0, unit)
            start_dots(field, 0, first, True)

            @pl.loop(0, chunks)
            def _(k):
                before(k)
                wait_halo(stage_in, k)

                @pl.loop(0, CHUNK // GROUP // 2)
                def _(i):
                    g = k * (CHUNK // GROUP) + 2 * i
                    one_group(g, first, second)
                    one_group(g + 1, second, first)
                if out is not None:
                    send_edges(stage_out, k)
                after(k)

            for acc in first:
                pltpu.matmul_pop(acc)

        pl.run_scoped(with_accumulators, *accumulators)

    def nothing(k):
        pass

    @pl.loop(0, chunks)
    def _(k):
        for yt in range(yt_n):
            state_copy(k, yt).wait()

        @pl.loop(0, CHUNK, unroll=4)
        def _(i):
            pack_edges(s2, 0, k * CHUNK + i)
        send_edges(0, k)

    above_copy.wait()
    below_copy.wait_recv()
    for xt in range(xt_n):
        for yt in range(yt_n):
            lo = below[(0,) + at(xt, yt)]
            hi = above[(0,) + at(xt, yt)]
            for field in (s2, m2):
                put(field, -1, xt, yt, lo)
                put(field, cz, xt, yt, hi)

    def middle(z, xt, yt, mid, lap):
        put(m2, z, xt, yt, mid + cf[(z,) + at(xt, yt)] * lap)

    sweep(s2, 0, middle, lambda k: coeff_copy(k).wait(), nothing, m2, 1)

    for xt in range(xt_n):
        for yt in range(yt_n):
            put(s2, -1, xt, yt, zero)
            put(s2, cz, xt, yt, zero)

    def finish(z, xt, yt, mid, lap):
        here = (z,) + at(xt, yt)
        c = cf[here]
        f = mid + c * lap
        final[here] = f
        two = f - tg[here]
        tg[here] = two
        put(s2, z, xt, yt, c * two)

    def send_trace(k):
        @pl.when(k == 0)
        def _():
            trace_copy.start()

    sweep(m2, 1, finish, lambda k: target_copy(k).wait(), send_trace, s2, 2)

    for xt in range(xt_n):
        for yt in range(yt_n):
            put(m2, -1, xt, yt, zero)
            put(m2, cz, xt, yt, zero)

    flux[0] = tg[0]
    top_two[0] = tg[cz - 1]

    def back_one(z, xt, yt, mid, lap):
        here = (z,) + at(xt, yt)
        one = tg[here] + lap
        tg[here] = one
        put(m2, z, xt, yt, cf[here] * one)

    def send_flux(k):
        @pl.when(k == 0)
        def _():
            flux[0] = cf[0] * (tg[0] + flux[0])
            flux_copy.start()

    sweep(s2, 2, back_one, nothing, send_flux, m2, 3)

    def back_two(z, xt, yt, mid, lap):
        here = (z,) + at(xt, yt)
        adj[here] = tg[here] + lap

    sweep(m2, 3, back_two, nothing, nothing)

    mult_copy.wait()
    trace_copy.wait_recv()
    flux_copy.wait_recv()
    nm = mult[0] + rho_step * (final[cz - 1] - low_trace[0])
    new_multiplier[0] = nm
    grad = cf[cz - 1] * (tg[cz - 1] + top_two[0]) + low_flux[0]
    new_control[0] = (above[0] - tau_step * (grad + nm)) / (1.0 + tau_step)

    below_copy.wait_send()
    trace_copy.wait_send()
    flux_copy.wait_send()
    for side in range(2):
        @pl.when(has[side])
        def _():
            for stage in range(4):
                @pl.loop(0, chunks)
                def _(k):
                    edge_copy(stage, side, k).wait_send()


def write_out(parts, *refs):
    sem = refs[-1]
    n = (len(refs) - 1) // 2
    copies = []
    for i in range(n):
        planes = refs[i].shape[0]
        step = max(planes // parts, 1)
        for j in range(planes // step):
            span = pl.ds(j * step, step)
            copies.append(pltpu.make_async_copy(refs[i].at[span], refs[n + i].at[span], sem.at[i, j]))
    for copy in copies:
        copy.start()
    for copy in copies:
        copy.wait()


def iterate(n_slab, n_tile, accumulators, state, coeff, target, control, multiplier):
    cz, nx, ny = state.shape
    yt_n = ny // LANES
    chunks = cz // CHUNK
    f32 = jnp.float32
    padded = pltpu.VMEM((cz + 3, yt_n, nx + SUB, LANES), f32)
    natural = pltpu.VMEM((cz, nx, ny), f32)
    sheet = pltpu.VMEM((1, nx, ny), f32)
    edges = pltpu.VMEM((4, 2, cz, yt_n, LANES), f32)
    dma = pltpu.SemaphoreType.DMA
    arrays = [pltpu.with_memory_space_constraint(a, pltpu.HBM) for a in (state, coeff, target, control, multiplier)]
    results = pl.pallas_call(
        functools.partial(kernel, cz, nx, ny, n_slab, n_tile, accumulators),
        out_shape=(natural, natural, sheet, sheet),
        in_specs=[pl.BlockSpec(memory_space=pltpu.HBM)] * 5,
        out_specs=[pl.BlockSpec(memory_space=pltpu.VMEM)] * 4,
        scratch_shapes=[padded, padded, natural, natural] + [sheet] * 7 + [edges, edges, pltpu.VMEM((2 * LANES, 2 * LANES), jnp.bfloat16)]
        + [dma((chunks, yt_n)), dma((chunks,)), dma((chunks,)), dma((2,)),
           dma((4, 2, chunks)), dma((4, 2, chunks)), dma((3,)), dma((3,))],
        compiler_params=pltpu.CompilerParams(
            collective_id=0, has_side_effects=True, vmem_limit_bytes=40 * 2**20),
    )(*arrays)
    full = jax.ShapeDtypeStruct((cz, nx, ny), f32)
    face = jax.ShapeDtypeStruct((1, nx, ny), f32)
    return pl.pallas_call(
        functools.partial(write_out, PARTS),
        out_shape=(full, full, face, face),
        in_specs=[pl.BlockSpec(memory_space=pltpu.VMEM)] * 4,
        out_specs=[pl.BlockSpec(memory_space=pl.ANY)] * 4,
        scratch_shapes=[dma((4, PARTS))],
        compiler_params=pltpu.CompilerParams(vmem_limit_bytes=16 * 2**20),
    )(*results)


def solution(mesh):
    spec = P("slab", "tile", None)
    with jax.sharding.use_abstract_mesh(mesh.abstract_mesh):
        count = 2 * BY_DOT * (NY // LANES)
        accumulators = [pltpu.ACC(mxu_id=i % UNITS)((NX_LOCAL, 2 * LANES), jnp.float32) for i in range(count)]
    run = functools.partial(iterate, mesh.shape["slab"], mesh.shape["tile"], accumulators)
    return jax.shard_map(run, mesh=mesh, in_specs=(spec,) * 5, out_specs=(spec,) * 4, check_vma=False)
```

```python
import functools

import jax
import jax.numpy as jnp
from jax import lax
from jax.experimental import pallas as pl
from jax.experimental.pallas import tpu as pltpu
from jax.sharding import PartitionSpec as P

rho_step = 0.5
tau_step = 0.5
LANES = 128
SUB = 8
CHUNK = 8
GROUP = 4
BY_DOT = 3
UNITS = 2
NY = 1024
NX_LOCAL = 16
MESH = pl.DeviceIdType.MESH


def nothing(_):
    pass


def tools(cz, nx, ny, accumulators, band):
    yt_n = ny // LANES
    xt_n = nx // SUB
    pitch = nx + SUB
    plane = yt_n * pitch
    chunks = cz // CHUNK
    lane = lax.broadcasted_iota(jnp.int32, (SUB, LANES), 1)
    first = lane == 0
    last = lane == LANES - 1
    zero = jnp.zeros((SUB, LANES), jnp.float32)

    def y_sums(field, z, xt):
        base = (z + 1) * plane + SUB + xt * SUB
        mid = [field[pl.ds(base + yt * pitch, SUB), :] for yt in range(yt_n)]
        right = [pltpu.roll(v, 1, 1) for v in mid]
        left = [pltpu.roll(v, LANES - 1, 1) for v in mid]
        return [jnp.where(first, right[yt - 1] if yt else zero, right[yt])
                + jnp.where(last, left[yt + 1] if yt + 1 < yt_n else zero, left[yt]) for yt in range(yt_n)]

    row = lax.rem(lax.broadcasted_iota(jnp.int32, (2 * LANES, LANES), 0), LANES)
    col = lax.broadcasted_iota(jnp.int32, (2 * LANES, LANES), 1)
    swap = jnp.logical_or(jnp.logical_and(row == LANES - 1, col == 0), jnp.logical_and(row == 0, col == LANES - 1))
    band[:, pl.ds(0, LANES)] = jnp.where(jnp.abs(row - col) == 1, 1.0, 0.0).astype(jnp.bfloat16)
    band[:, pl.ds(LANES, LANES)] = jnp.where(swap, 1.0, 0.0).astype(jnp.bfloat16)
    lower_half = lax.broadcasted_iota(jnp.int32, (nx, LANES), 1) < LANES // 2
    no_piece = jnp.zeros((nx, LANES), jnp.float32)

    def start_dots(field, z, accs, load=False):
        for p in range(BY_DOT):
            base = (z + p + 1) * plane + SUB
            for yt in range(yt_n):
                mid = field[pl.ds(base + yt * pitch, nx), :]
                high = mid.astype(jnp.bfloat16)
                low = (mid - high.astype(jnp.float32)).astype(jnp.bfloat16)
                pltpu.matmul_acc_lhs(accs[p * yt_n + yt], jnp.concatenate([high, low], axis=1),
                                     load_staged_rhs=0 if load and p * yt_n + yt < UNITS else None)

    def take_dots(accs, p):
        both = [pltpu.matmul_pop(accs[p * yt_n + yt]) for yt in range(yt_n)]
        sums = []
        for yt in range(yt_n):
            lower = both[yt - 1][:, LANES:] if yt else no_piece
            upper = both[yt + 1][:, LANES:] if yt + 1 < yt_n else no_piece
            sums.append(both[yt][:, :LANES] + jnp.where(lower_half, lower, upper))
        return [[v[xt * SUB:(xt + 1) * SUB] for v in sums] for xt in range(xt_n)]

    def put(field, z, xt, yt, value):
        field[pl.ds((z + 1) * plane + SUB + xt * SUB + yt * pitch, SUB), :] = value

    def at(xt, yt):
        return pl.ds(xt * SUB, SUB), pl.ds(yt * LANES, LANES)

    groups = cz // GROUP

    def sweep(field, emit, before, after, place=nothing, pack=nothing):
        def one_group(g, have, make):
            z = g * GROUP
            for p in range(GROUP):
                place(z + p)
            start_dots(field, lax.rem(g + 1, groups) * GROUP, make)
            for p in range(GROUP):
                if p < BY_DOT:
                    sums = take_dots(have, p)
                else:
                    sums = [y_sums(field, z + p, xt) for xt in range(xt_n)]
                for yt in range(yt_n):
                    for xt in range(xt_n):
                        at = (z + p + 1) * plane + SUB + xt * SUB + yt * pitch
                        mid = field[pl.ds(at, SUB), :]
                        x_sum = field[pl.ds(at + 1, SUB), :] + field[pl.ds(at - 1, SUB), :]
                        z_sum = field[pl.ds(at + plane, SUB), :] + field[pl.ds(at - plane, SUB), :]
                        emit(z + p, xt, yt, mid, (z_sum + x_sum) + sums[xt][yt] - 6.0 * mid)
            for p in range(GROUP):
                pack(z + p)

        def with_accumulators(*accs):
            first, second = accs[:BY_DOT * yt_n], accs[BY_DOT * yt_n:]
            for unit in range(UNITS):
                pltpu.matmul_push_rhs(band[...], 0, unit)
            start_dots(field, 0, first, True)

            @pl.loop(0, chunks)
            def _(k):
                before(k)

                @pl.loop(0, CHUNK // GROUP // 2)
                def _(i):
                    g = k * (CHUNK // GROUP) + 2 * i
                    one_group(g, first, second)
                    one_group(g + 1, second, first)
                after(k)

            for acc in first:
                pltpu.matmul_pop(acc)

        pl.run_scoped(with_accumulators, *accumulators)

    return sweep, put, at, zero


def kernel(cz, nx, ny, n_slab, n_tile, accumulators,
           state, coeff, target, control, multiplier,
           final, tg, mp, new_control, new_multiplier,
           sp, cf, above, mult, below, flux, top_two, low_trace, low_flux,
           send, recv, band,
           sem_state, sem_coeff, sem_target, sem_small, sem_send, sem_recv, sem_slab_send, sem_slab_recv):
    yt_n = ny // LANES
    xt_n = nx // SUB
    pitch = nx + SUB
    plane = yt_n * pitch
    chunks = cz // CHUNK
    rows_n = sp.shape[0] * plane
    s2 = sp.reshape(rows_n, LANES)
    m2 = mp.reshape(rows_n, LANES)

    slab = lax.axis_index("slab")
    tile = lax.axis_index("tile")
    has = (tile > 0, tile < n_tile - 1)
    side_dev = ((slab, jnp.maximum(tile - 1, 0)), (slab, jnp.minimum(tile + 1, n_tile - 1)))
    up = (lax.rem(slab + 1, n_slab), tile)
    down = (lax.rem(slab + n_slab - 1, n_slab), tile)

    barrier = pltpu.get_barrier_semaphore()
    for side in range(2):
        @pl.when(has[side])
        def _():
            pl.semaphore_signal(barrier, inc=1, device_id=side_dev[side], device_id_type=MESH)
    pl.semaphore_signal(barrier, inc=1, device_id=up, device_id_type=MESH)
    pl.semaphore_signal(barrier, inc=1, device_id=down, device_id_type=MESH)

    def state_copy(k, yt):
        return pltpu.make_async_copy(
            state.at[pl.ds(k * CHUNK, CHUNK), :, pl.ds(yt * LANES, LANES)],
            sp.at[pl.ds(k * CHUNK + 1, CHUNK), yt, pl.ds(SUB, nx), :],
            sem_state.at[k, yt])

    def coeff_copy(k):
        return pltpu.make_async_copy(
            coeff.at[pl.ds(k * CHUNK, CHUNK)], cf.at[pl.ds(k * CHUNK, CHUNK)], sem_coeff.at[k])

    def target_copy(k):
        return pltpu.make_async_copy(
            target.at[pl.ds(k * CHUNK, CHUNK)], tg.at[pl.ds(k * CHUNK, CHUNK)], sem_target.at[k])

    above_copy = pltpu.make_async_copy(control, above, sem_small.at[0])
    mult_copy = pltpu.make_async_copy(multiplier, mult, sem_small.at[1])

    @pl.loop(0, chunks)
    def _(k):
        for yt in range(yt_n):
            state_copy(k, yt).start()
    above_copy.start()

    @pl.loop(0, chunks)
    def _(k):
        coeff_copy(k).start()

    @pl.loop(0, chunks)
    def _(k):
        target_copy(k).start()
    mult_copy.start()

    for side in range(2):
        @pl.when(jnp.logical_not(has[side]))
        def _():
            @pl.loop(0, cz)
            def _(z):
                for stage in range(4):
                    recv[stage, side, z] = jnp.zeros((yt_n, LANES), jnp.float32)

    pl.semaphore_wait(barrier, 2 + has[0].astype(jnp.int32) + has[1].astype(jnp.int32))

    def slab_copy(i, src, dst, dev):
        return pltpu.make_async_remote_copy(
            src_ref=src, dst_ref=dst, send_sem=sem_slab_send.at[i], recv_sem=sem_slab_recv.at[i],
            device_id=dev, device_id_type=MESH)

    below_copy = slab_copy(0, control, below, up)
    trace_copy = slab_copy(1, final.at[pl.ds(0, 1)], low_trace, down)
    flux_copy = slab_copy(2, flux, low_flux, down)
    below_copy.start()

    def edge_copy(stage, side, k):
        return pltpu.make_async_remote_copy(
            src_ref=send.at[stage, side, pl.ds(k * CHUNK, CHUNK)],
            dst_ref=recv.at[stage, 1 - side, pl.ds(k * CHUNK, CHUNK)],
            send_sem=sem_send.at[stage, side], recv_sem=sem_recv.at[stage, 1 - side, k],
            device_id=side_dev[side], device_id_type=MESH)

    def all_edges(stage, side):
        return pltpu.make_async_remote_copy(
            src_ref=send.at[stage, side], dst_ref=recv.at[stage, 1 - side],
            send_sem=sem_send.at[stage, side], recv_sem=sem_recv.at[stage, 1 - side, 0],
            device_id=side_dev[side], device_id_type=MESH)

    def pack_edges(field, stage, z):
        base = (z + 1) * plane
        send[stage, 0, z] = field[pl.ds(base + SUB, yt_n, stride=pitch), :]
        send[stage, 1, z] = field[pl.ds(base + SUB + nx - 1, yt_n, stride=pitch), :]

    def send_edges(stage, k):
        for side in range(2):
            @pl.when(has[side])
            def _():
                edge_copy(stage, side, k).start()

    def wait_halo(stage, k):
        for side in range(2):
            @pl.when(has[side])
            def _():
                edge_copy(stage, 1 - side, k).wait_recv()

    def stage(field, number, emit, out, before=nothing, after=nothing):
        def start(k):
            before(k)
            wait_halo(number, k)

        def end(k):
            send_edges(number + 1, k)
            after(k)
        sweep(field, emit, start, end, lambda z: place_halo(field, number, z), lambda z: pack_edges(out, number + 1, z))

    def place_halo(field, stage, z):
        base = (z + 1) * plane
        field[pl.ds(base + SUB - 1, yt_n, stride=pitch), :] = recv[stage, 0, z]
        field[pl.ds(base + SUB + nx, yt_n, stride=pitch), :] = recv[stage, 1, z]

    sweep, put, at, zero = tools(cz, nx, ny, accumulators, band)

    @pl.loop(0, chunks)
    def _(k):
        for yt in range(yt_n):
            state_copy(k, yt).wait()

        @pl.loop(0, CHUNK, unroll=4)
        def _(i):
            pack_edges(s2, 0, k * CHUNK + i)
        send_edges(0, k)

    above_copy.wait()
    below_copy.wait_recv()
    for xt in range(xt_n):
        for yt in range(yt_n):
            lo = below[(0,) + at(xt, yt)]
            hi = above[(0,) + at(xt, yt)]
            for field in (s2, m2):
                put(field, -1, xt, yt, lo)
                put(field, cz, xt, yt, hi)

    def middle(z, xt, yt, mid, lap):
        put(m2, z, xt, yt, mid + cf[(z,) + at(xt, yt)] * lap)

    stage(s2, 0, middle, m2, lambda k: coeff_copy(k).wait())

    for xt in range(xt_n):
        for yt in range(yt_n):
            put(s2, -1, xt, yt, zero)
            put(s2, cz, xt, yt, zero)

    def finish(z, xt, yt, mid, lap):
        here = (z,) + at(xt, yt)
        c = cf[here]
        f = mid + c * lap
        final[here] = f
        two = f - tg[here]
        tg[here] = two
        put(s2, z, xt, yt, c * two)

    def send_trace(k):
        @pl.when(k == 0)
        def _():
            trace_copy.start()

    stage(m2, 1, finish, s2, lambda k: target_copy(k).wait(), send_trace)

    for xt in range(xt_n):
        for yt in range(yt_n):
            put(m2, -1, xt, yt, zero)
            put(m2, cz, xt, yt, zero)

    flux[0] = tg[0]
    top_two[0] = tg[cz - 1]

    def back_one(z, xt, yt, mid, lap):
        here = (z,) + at(xt, yt)
        one = tg[here] + lap
        tg[here] = one
        put(m2, z, xt, yt, cf[here] * one)

    def send_flux(k):
        @pl.when(k == 0)
        def _():
            flux[0] = cf[0] * (tg[0] + flux[0])
            flux_copy.start()

    stage(s2, 2, back_one, m2, nothing, send_flux)

    mult_copy.wait()
    trace_copy.wait_recv()
    flux_copy.wait_recv()
    nm = mult[0] + rho_step * (final[cz - 1] - low_trace[0])
    new_multiplier[0] = nm
    grad = cf[cz - 1] * (tg[cz - 1] + top_two[0]) + low_flux[0]
    new_control[0] = (above[0] - tau_step * (grad + nm)) / (1.0 + tau_step)

    below_copy.wait_send()
    trace_copy.wait_send()
    flux_copy.wait_send()
    @pl.loop(0, chunks)
    def _(k):
        wait_halo(3, k)
        for i in range(CHUNK):
            place_halo(m2, 3, k * CHUNK + i)

    for side in range(2):
        @pl.when(has[side])
        def _():
            for number in range(4):
                all_edges(number, side).wait_send()


def last_stage(cz, nx, ny, accumulators,
               final, tg, mp, control, multiplier, final_out, adj_out, control_out, multiplier_out,
               adj, band, sem, sem_adj):
    copies = [pltpu.make_async_copy(a, b, sem.at[i]) for i, (a, b) in enumerate(
        ((final, final_out), (control, control_out), (multiplier, multiplier_out)))]
    for copy in copies:
        copy.start()
    m2 = mp.reshape(mp.shape[0] * (ny // LANES) * (nx + SUB), LANES)
    sweep, _, at, _ = tools(cz, nx, ny, accumulators, band)

    def adj_copy(k):
        planes = pl.ds(k * CHUNK, CHUNK)
        return pltpu.make_async_copy(adj.at[planes], adj_out.at[planes], sem_adj.at[k])

    def back_two(z, xt, yt, mid, lap):
        here = (z,) + at(xt, yt)
        adj[here] = tg[here] + lap

    sweep(m2, back_two, nothing, lambda k: adj_copy(k).start())
    for copy in copies:
        copy.wait()

    @pl.loop(0, cz // CHUNK)
    def _(k):
        adj_copy(k).wait()


def iterate(n_slab, n_tile, accumulators, state, coeff, target, control, multiplier):
    cz, nx, ny = state.shape
    yt_n = ny // LANES
    chunks = cz // CHUNK
    f32 = jnp.float32
    padded = pltpu.VMEM((cz + 3, yt_n, nx + SUB, LANES), f32)
    natural = pltpu.VMEM((cz, nx, ny), f32)
    sheet = pltpu.VMEM((1, nx, ny), f32)
    edges = pltpu.VMEM((4, 2, cz, yt_n, LANES), f32)
    dma = pltpu.SemaphoreType.DMA
    arrays = [pltpu.with_memory_space_constraint(a, pltpu.HBM) for a in (state, coeff, target, control, multiplier)]
    results = pl.pallas_call(
        functools.partial(kernel, cz, nx, ny, n_slab, n_tile, accumulators),
        out_shape=(natural, natural, padded, sheet, sheet),
        in_specs=[pl.BlockSpec(memory_space=pltpu.HBM)] * 5,
        out_specs=[pl.BlockSpec(memory_space=pltpu.VMEM)] * 5,
        scratch_shapes=[padded, natural] + [sheet] * 7 + [edges, edges, pltpu.VMEM((2 * LANES, 2 * LANES), jnp.bfloat16)]
        + [dma((chunks, yt_n)), dma((chunks,)), dma((chunks,)), dma((2,)),
           dma((4, 2)), dma((4, 2, chunks)), dma((3,)), dma((3,))],
        compiler_params=pltpu.CompilerParams(
            collective_id=0, has_side_effects=True, vmem_limit_bytes=32 * 2**20),
    )(*arrays)
    full = jax.ShapeDtypeStruct((cz, nx, ny), f32)
    face = jax.ShapeDtypeStruct((1, nx, ny), f32)
    return pl.pallas_call(
        functools.partial(last_stage, cz, nx, ny, accumulators),
        out_shape=(full, full, face, face),
        in_specs=[pl.BlockSpec(memory_space=pltpu.VMEM)] * 5,
        out_specs=[pl.BlockSpec(memory_space=pl.ANY)] * 4,
        scratch_shapes=[natural, pltpu.VMEM((2 * LANES, 2 * LANES), jnp.bfloat16), dma((3,)), dma((chunks,))],
        compiler_params=pltpu.CompilerParams(vmem_limit_bytes=16 * 2**20),
    )(*results)


def solution(mesh):
    spec = P("slab", "tile", None)
    with jax.sharding.use_abstract_mesh(mesh.abstract_mesh):
        count = 2 * BY_DOT * (NY // LANES)
        accumulators = [pltpu.ACC(mxu_id=i % UNITS)((NX_LOCAL, 2 * LANES), jnp.float32) for i in range(count)]
    run = functools.partial(iterate, mesh.shape["slab"], mesh.shape["tile"], accumulators)
    return jax.shard_map(run, mesh=mesh, in_specs=(spec,) * 5, out_specs=(spec,) * 4, check_vma=False)
```

```python
import functools

import jax
import jax.numpy as jnp
from jax import lax
from jax.experimental import pallas as pl
from jax.experimental.pallas import tpu as pltpu
from jax.sharding import PartitionSpec as P

rho_step = 0.5
tau_step = 0.5
LANES = 128
SUB = 8
CHUNK = 8
GROUP = 4
UNITS = 2
NY = 1024
NX_LOCAL = 16
MESH = pl.DeviceIdType.MESH


def nothing(_):
    pass


def tools(cz, nx, ny, accumulators, band):
    yt_n = ny // LANES
    xt_n = nx // SUB
    pitch = nx + SUB
    plane = yt_n * pitch
    chunks = cz // CHUNK
    zero = jnp.zeros((SUB, LANES), jnp.float32)

    row = lax.rem(lax.broadcasted_iota(jnp.int32, (2 * LANES, LANES), 0), LANES)
    col = lax.broadcasted_iota(jnp.int32, (2 * LANES, LANES), 1)
    swap = jnp.logical_or(jnp.logical_and(row == LANES - 1, col == 0), jnp.logical_and(row == 0, col == LANES - 1))
    band[:, pl.ds(0, LANES)] = jnp.where(jnp.abs(row - col) == 1, 1.0, 0.0).astype(jnp.bfloat16)
    band[:, pl.ds(LANES, LANES)] = jnp.where(swap, 1.0, 0.0).astype(jnp.bfloat16)
    lower_half = lax.broadcasted_iota(jnp.int32, (nx, LANES), 1) < LANES // 2
    no_piece = jnp.zeros((nx, LANES), jnp.float32)

    def start_dots(field, z, accs, load=False):
        for p in range(GROUP):
            base = (z + p + 1) * plane + SUB
            for yt in range(yt_n):
                mid = field[pl.ds(base + yt * pitch, nx), :]
                high = mid.astype(jnp.bfloat16)
                low = (mid - high.astype(jnp.float32)).astype(jnp.bfloat16)
                pltpu.matmul_acc_lhs(accs[p * yt_n + yt], jnp.concatenate([high, low], axis=1),
                                     load_staged_rhs=0 if load and p * yt_n + yt < UNITS else None)

    def take_dots(accs, p):
        before, here = no_piece, pltpu.matmul_pop(accs[p * yt_n])
        for yt in range(yt_n):
            behind = pltpu.matmul_pop(accs[p * yt_n + yt + 1]) if yt + 1 < yt_n else None
            upper = no_piece if behind is None else behind[:, LANES:]
            sums = here[:, :LANES] + jnp.where(lower_half, before, upper)
            yield [sums[xt * SUB:(xt + 1) * SUB] for xt in range(xt_n)]
            before, here = here[:, LANES:], behind

    def put(field, z, xt, yt, value):
        field[pl.ds((z + 1) * plane + SUB + xt * SUB + yt * pitch, SUB), :] = value

    def at(xt, yt):
        return pl.ds(xt * SUB, SUB), pl.ds(yt * LANES, LANES)

    groups = cz // GROUP

    def sweep(field, emit, before, after, place=nothing, pack=nothing):
        def one_group(g, have, make):
            z = g * GROUP
            for p in range(GROUP):
                place(z + p)
            start_dots(field, lax.rem(g + 1, groups) * GROUP, make)
            for p in range(GROUP):
                for yt, sums in enumerate(take_dots(have, p)):
                    for xt in range(xt_n):
                        at = (z + p + 1) * plane + SUB + xt * SUB + yt * pitch
                        mid = field[pl.ds(at, SUB), :]
                        x_sum = field[pl.ds(at + 1, SUB), :] + field[pl.ds(at - 1, SUB), :]
                        z_sum = field[pl.ds(at + plane, SUB), :] + field[pl.ds(at - plane, SUB), :]
                        emit(z + p, xt, yt, mid, (z_sum + x_sum) + sums[xt] - 6.0 * mid)
            for p in range(GROUP):
                pack(z + p)

        def with_accumulators(*accs):
            first, second = accs[:GROUP * yt_n], accs[GROUP * yt_n:]
            for unit in range(UNITS):
                pltpu.matmul_push_rhs(band[...], 0, unit)
            start_dots(field, 0, first, True)

            @pl.loop(0, chunks)
            def _(k):
                before(k)

                @pl.loop(0, CHUNK // GROUP // 2)
                def _(i):
                    g = k * (CHUNK // GROUP) + 2 * i
                    one_group(g, first, second)
                    one_group(g + 1, second, first)
                after(k)

            for acc in first:
                pltpu.matmul_pop(acc)

        pl.run_scoped(with_accumulators, *accumulators)

    return sweep, put, at, zero


def kernel(cz, nx, ny, n_slab, n_tile, accumulators,
           state, coeff, target, control, multiplier,
           final, tg, mp, new_control, new_multiplier,
           sp, cf, above, mult, below, flux, top_two, low_trace, low_flux,
           send, recv, band,
           sem_state, sem_coeff, sem_target, sem_small, sem_send, sem_recv, sem_slab_send, sem_slab_recv):
    yt_n = ny // LANES
    xt_n = nx // SUB
    pitch = nx + SUB
    plane = yt_n * pitch
    chunks = cz // CHUNK
    rows_n = sp.shape[0] * plane
    s2 = sp.reshape(rows_n, LANES)
    m2 = mp.reshape(rows_n, LANES)

    slab = lax.axis_index("slab")
    tile = lax.axis_index("tile")
    has = (tile > 0, tile < n_tile - 1)
    side_dev = ((slab, jnp.maximum(tile - 1, 0)), (slab, jnp.minimum(tile + 1, n_tile - 1)))
    up = (lax.rem(slab + 1, n_slab), tile)
    down = (lax.rem(slab + n_slab - 1, n_slab), tile)

    barrier = pltpu.get_barrier_semaphore()
    for side in range(2):
        @pl.when(has[side])
        def _():
            pl.semaphore_signal(barrier, inc=1, device_id=side_dev[side], device_id_type=MESH)
    pl.semaphore_signal(barrier, inc=1, device_id=up, device_id_type=MESH)
    pl.semaphore_signal(barrier, inc=1, device_id=down, device_id_type=MESH)

    def state_copy(k, yt):
        return pltpu.make_async_copy(
            state.at[pl.ds(k * CHUNK, CHUNK), :, pl.ds(yt * LANES, LANES)],
            sp.at[pl.ds(k * CHUNK + 1, CHUNK), yt, pl.ds(SUB, nx), :],
            sem_state.at[k, yt])

    def coeff_copy(k):
        return pltpu.make_async_copy(
            coeff.at[pl.ds(k * CHUNK, CHUNK)], cf.at[pl.ds(k * CHUNK, CHUNK)], sem_coeff.at[k])

    def target_copy(k):
        return pltpu.make_async_copy(
            target.at[pl.ds(k * CHUNK, CHUNK)], tg.at[pl.ds(k * CHUNK, CHUNK)], sem_target.at[k])

    above_copy = pltpu.make_async_copy(control, above, sem_small.at[0])
    mult_copy = pltpu.make_async_copy(multiplier, mult, sem_small.at[1])

    @pl.loop(0, chunks)
    def _(k):
        for yt in range(yt_n):
            state_copy(k, yt).start()
    above_copy.start()

    @pl.loop(0, chunks)
    def _(k):
        coeff_copy(k).start()

    @pl.loop(0, chunks)
    def _(k):
        target_copy(k).start()
    mult_copy.start()

    for side in range(2):
        @pl.when(jnp.logical_not(has[side]))
        def _():
            @pl.loop(0, cz)
            def _(z):
                for stage in range(4):
                    recv[stage, side, z] = jnp.zeros((yt_n, LANES), jnp.float32)

    pl.semaphore_wait(barrier, 2 + has[0].astype(jnp.int32) + has[1].astype(jnp.int32))

    def slab_copy(i, src, dst, dev):
        return pltpu.make_async_remote_copy(
            src_ref=src, dst_ref=dst, send_sem=sem_slab_send.at[i], recv_sem=sem_slab_recv.at[i],
            device_id=dev, device_id_type=MESH)

    below_copy = slab_copy(0, control, below, up)
    trace_copy = slab_copy(1, final.at[pl.ds(0, 1)], low_trace, down)
    flux_copy = slab_copy(2, flux, low_flux, down)
    below_copy.start()

    def edge_copy(stage, side, k):
        return pltpu.make_async_remote_copy(
            src_ref=send.at[stage, side, pl.ds(k * CHUNK, CHUNK)],
            dst_ref=recv.at[stage, 1 - side, pl.ds(k * CHUNK, CHUNK)],
            send_sem=sem_send.at[stage, side], recv_sem=sem_recv.at[stage, 1 - side, k],
            device_id=side_dev[side], device_id_type=MESH)

    def all_edges(stage, side):
        return pltpu.make_async_remote_copy(
            src_ref=send.at[stage, side], dst_ref=recv.at[stage, 1 - side],
            send_sem=sem_send.at[stage, side], recv_sem=sem_recv.at[stage, 1 - side, 0],
            device_id=side_dev[side], device_id_type=MESH)

    def pack_edges(field, stage, z):
        base = (z + 1) * plane
        send[stage, 0, z] = field[pl.ds(base + SUB, yt_n, stride=pitch), :]
        send[stage, 1, z] = field[pl.ds(base + SUB + nx - 1, yt_n, stride=pitch), :]

    def send_edges(stage, k):
        for side in range(2):
            @pl.when(has[side])
            def _():
                edge_copy(stage, side, k).start()

    def wait_halo(stage, k):
        for side in range(2):
            @pl.when(has[side])
            def _():
                edge_copy(stage, 1 - side, k).wait_recv()

    def stage(field, number, emit, out, before=nothing, after=nothing):
        def start(k):
            before(k)
            wait_halo(number, k)

        def end(k):
            send_edges(number + 1, k)
            after(k)
        sweep(field, emit, start, end, lambda z: place_halo(field, number, z), lambda z: pack_edges(out, number + 1, z))

    def place_halo(field, stage, z):
        base = (z + 1) * plane
        field[pl.ds(base + SUB - 1, yt_n, stride=pitch), :] = recv[stage, 0, z]
        field[pl.ds(base + SUB + nx, yt_n, stride=pitch), :] = recv[stage, 1, z]

    sweep, put, at, zero = tools(cz, nx, ny, accumulators, band)

    @pl.loop(0, chunks)
    def _(k):
        for yt in range(yt_n):
            state_copy(k, yt).wait()

        @pl.loop(0, CHUNK, unroll=4)
        def _(i):
            pack_edges(s2, 0, k * CHUNK + i)
        send_edges(0, k)

    above_copy.wait()
    below_copy.wait_recv()
    for xt in range(xt_n):
        for yt in range(yt_n):
            lo = below[(0,) + at(xt, yt)]
            hi = above[(0,) + at(xt, yt)]
            for field in (s2, m2):
                put(field, -1, xt, yt, lo)
                put(field, cz, xt, yt, hi)

    def middle(z, xt, yt, mid, lap):
        put(m2, z, xt, yt, mid + cf[(z,) + at(xt, yt)] * lap)

    stage(s2, 0, middle, m2, lambda k: coeff_copy(k).wait())

    for xt in range(xt_n):
        for yt in range(yt_n):
            put(s2, -1, xt, yt, zero)
            put(s2, cz, xt, yt, zero)

    def finish(z, xt, yt, mid, lap):
        here = (z,) + at(xt, yt)
        c = cf[here]
        f = mid + c * lap
        final[here] = f
        two = f - tg[here]
        tg[here] = two
        put(s2, z, xt, yt, c * two)

    def send_trace(k):
        @pl.when(k == 0)
        def _():
            trace_copy.start()

    stage(m2, 1, finish, s2, lambda k: target_copy(k).wait(), send_trace)

    for xt in range(xt_n):
        for yt in range(yt_n):
            put(m2, -1, xt, yt, zero)
            put(m2, cz, xt, yt, zero)

    flux[0] = tg[0]
    top_two[0] = tg[cz - 1]

    def back_one(z, xt, yt, mid, lap):
        here = (z,) + at(xt, yt)
        one = tg[here] + lap
        tg[here] = one
        put(m2, z, xt, yt, cf[here] * one)

    def send_flux(k):
        @pl.when(k == 0)
        def _():
            flux[0] = cf[0] * (tg[0] + flux[0])
            flux_copy.start()

    stage(s2, 2, back_one, m2, nothing, send_flux)

    mult_copy.wait()
    trace_copy.wait_recv()
    flux_copy.wait_recv()
    nm = mult[0] + rho_step * (final[cz - 1] - low_trace[0])
    new_multiplier[0] = nm
    grad = cf[cz - 1] * (tg[cz - 1] + top_two[0]) + low_flux[0]
    new_control[0] = (above[0] - tau_step * (grad + nm)) / (1.0 + tau_step)

    below_copy.wait_send()
    trace_copy.wait_send()
    flux_copy.wait_send()
    @pl.loop(0, chunks)
    def _(k):
        wait_halo(3, k)
        for i in range(CHUNK):
            place_halo(m2, 3, k * CHUNK + i)

    for side in range(2):
        @pl.when(has[side])
        def _():
            for number in range(4):
                all_edges(number, side).wait_send()


def last_stage(cz, nx, ny, accumulators,
               final, tg, mp, control, multiplier, final_out, adj_out, control_out, multiplier_out,
               adj, band, sem, sem_adj):
    copies = [pltpu.make_async_copy(a, b, sem.at[i]) for i, (a, b) in enumerate(
        ((final, final_out), (control, control_out), (multiplier, multiplier_out)))]
    for copy in copies:
        copy.start()
    m2 = mp.reshape(mp.shape[0] * (ny // LANES) * (nx + SUB), LANES)
    sweep, _, at, _ = tools(cz, nx, ny, accumulators, band)

    def adj_copy(k):
        planes = pl.ds(k * CHUNK, CHUNK)
        return pltpu.make_async_copy(adj.at[planes], adj_out.at[planes], sem_adj.at[k])

    def back_two(z, xt, yt, mid, lap):
        here = (z,) + at(xt, yt)
        adj[here] = tg[here] + lap

    sweep(m2, back_two, nothing, lambda k: adj_copy(k).start())
    for copy in copies:
        copy.wait()

    @pl.loop(0, cz // CHUNK)
    def _(k):
        adj_copy(k).wait()


def iterate(n_slab, n_tile, accumulators, state, coeff, target, control, multiplier):
    cz, nx, ny = state.shape
    yt_n = ny // LANES
    chunks = cz // CHUNK
    f32 = jnp.float32
    padded = pltpu.VMEM((cz + 3, yt_n, nx + SUB, LANES), f32)
    natural = pltpu.VMEM((cz, nx, ny), f32)
    sheet = pltpu.VMEM((1, nx, ny), f32)
    edges = pltpu.VMEM((4, 2, cz, yt_n, LANES), f32)
    dma = pltpu.SemaphoreType.DMA
    arrays = [pltpu.with_memory_space_constraint(a, pltpu.HBM) for a in (state, coeff, target, control, multiplier)]
    results = pl.pallas_call(
        functools.partial(kernel, cz, nx, ny, n_slab, n_tile, accumulators),
        out_shape=(natural, natural, padded, sheet, sheet),
        in_specs=[pl.BlockSpec(memory_space=pltpu.HBM)] * 5,
        out_specs=[pl.BlockSpec(memory_space=pltpu.VMEM)] * 5,
        scratch_shapes=[padded, natural] + [sheet] * 7 + [edges, edges, pltpu.VMEM((2 * LANES, 2 * LANES), jnp.bfloat16)]
        + [dma((chunks, yt_n)), dma((chunks,)), dma((chunks,)), dma((2,)),
           dma((4, 2)), dma((4, 2, chunks)), dma((3,)), dma((3,))],
        compiler_params=pltpu.CompilerParams(
            collective_id=0, has_side_effects=True, vmem_limit_bytes=32 * 2**20),
    )(*arrays)
    full = jax.ShapeDtypeStruct((cz, nx, ny), f32)
    face = jax.ShapeDtypeStruct((1, nx, ny), f32)
    return pl.pallas_call(
        functools.partial(last_stage, cz, nx, ny, accumulators),
        out_shape=(full, full, face, face),
        in_specs=[pl.BlockSpec(memory_space=pltpu.VMEM)] * 5,
        out_specs=[pl.BlockSpec(memory_space=pl.ANY)] * 4,
        scratch_shapes=[natural, pltpu.VMEM((2 * LANES, 2 * LANES), jnp.bfloat16), dma((3,)), dma((chunks,))],
        compiler_params=pltpu.CompilerParams(vmem_limit_bytes=16 * 2**20),
    )(*results)


def solution(mesh):
    spec = P("slab", "tile", None)
    with jax.sharding.use_abstract_mesh(mesh.abstract_mesh):
        count = 2 * GROUP * (NY // LANES)
        accumulators = [pltpu.ACC(mxu_id=i % UNITS)((NX_LOCAL, 2 * LANES), jnp.float32) for i in range(count)]
    run = functools.partial(iterate, mesh.shape["slab"], mesh.shape["tile"], accumulators)
    return jax.shard_map(run, mesh=mesh, in_specs=(spec,) * 5, out_specs=(spec,) * 4, check_vma=False)
```
